256 devices in a mesh: row: 8 (over x, core), col: 4 (over z_lo), layer: 8 (over y, z_hi).
Axes of the slice: x: 4, y: 4, z: 8 (z_hi: 2, z_lo: 4; z = z_hi * 4 + z_lo), core: 2. Of those that a mesh axis runs over, the one named last changes fastest.
Arguments:
- a_tiles: bfloat16 [8192, 16384], P('row', ('layer', 'col')), may hold values from -6 to 6
- a_occupancy: int32 [64, 128], P('row', ('layer', 'col')), may hold values 0 or 1
- b_tiles: bfloat16 [16384, 8192], P(('layer', 'row'), 'col'), may hold values from -0.046875 to 0.046875
- b_occupancy: int32 [128, 64], P(('layer', 'row'), 'col'), may hold values 0 or 1
Outputs:
- product: float32 [8192, 8192], P(('row', 'layer'), 'col')
The draws below stay inside these ranges and needn't reach their ends.
Inputs may be any that keep to these rules, and one draw needn't show every extreme that they name: `a_occupancy`: each entry is 0 (block absent) or 1 (block present). `b_occupancy`: each entry is 0 (block absent) or 1 (block present).
All inputs are finite; a program needn't handle non-finite values.
Results may differ from the reference program's by a relative error of at most 0.0003.
Values may be sent and summed in bfloat16 or wider, within the bound.
A program may use at most 64 MiB of HBM per device.

```python
import jax
import jax.numpy as jnp

BLOCK = 128
INNER = 16384
M_ROWS = 8192
N_COLS = 8192


def place_ends(entries, own_key, low, high):
    longest = entries.shape.index(max(entries.shape))
    spots = []
    for shift in (0, 1):
        where = [jax.random.randint(jax.random.fold_in(own_key, axis), (), 0, length) for axis, length in enumerate(entries.shape)]
        where[longest] = (where[longest] + shift) % entries.shape[longest]
        spots.append(tuple(where))
    return entries.at[spots[0]].set(low).at[spots[1]].set(high)


def level_of(key, dims, split, least, top_value):
    factor_of = 1.0
    for dim, parts in split:
        heights = jax.random.uniform(jax.random.fold_in(jax.random.fold_in(key, 6), dim), (parts,), jnp.float32, least / len(split), top_value / len(split))
        factor_of = factor_of * jnp.repeat(jnp.exp(heights), dims[dim] // parts).reshape((-1,) + (1,) * (len(dims) - 1 - dim))
    return factor_of


def centred(key, extent, spread, most, cuts=(), kind=jnp.bfloat16):
    entries = spread * jax.random.normal(key, extent, jnp.float32)
    if cuts:
        entries = entries * level_of(key, extent, cuts, -0.22, 0.18)
    return jnp.clip(entries, -most, most).astype(kind)


def setup_inputs(seed: int = 0) -> dict:
    arg_keys = jax.random.split(jax.random.key(seed), 5)
    return {
        "a_tiles": centred(arg_keys[0], (M_ROWS, INNER), 1.0, 6.0, ((0, 8), (1, 32))),
        "a_occupancy": place_ends((jax.random.randint(arg_keys[1], (M_ROWS // BLOCK, INNER // BLOCK), 0, 25) < 11).astype(jnp.int32), jax.random.fold_in(arg_keys[1], 1), 0, 1),
        "b_tiles": centred(arg_keys[2], (INNER, N_COLS), INNER ** -0.5, 0.046875, ((0, 64), (1, 4))),
        "b_occupancy": place_ends((jax.random.randint(arg_keys[3], (INNER // BLOCK, N_COLS // BLOCK), 0, 25) < 11).astype(jnp.int32), jax.random.fold_in(arg_keys[3], 1), 0, 1),
    }


def keep_blocks(values, occupancy):
    height, breadth = values.shape
    tiled = values.reshape(height // BLOCK, BLOCK, breadth // BLOCK, BLOCK)
    flags = occupancy.astype(values.dtype)
    return (tiled * flags[:, None, :, None]).reshape(height, breadth)


def reference(a_tiles, a_occupancy, b_tiles, b_occupancy):
    a_kept = keep_blocks(a_tiles, a_occupancy)
    b_kept = keep_blocks(b_tiles, b_occupancy)
    return jnp.dot(a_kept, b_kept, preferred_element_type=jnp.float32)
```

```python
import functools

import jax
import jax.numpy as jnp
from jax import lax
from jax.experimental import pallas as pl
from jax.experimental.pallas import tpu as pltpu
from jax.sharding import PartitionSpec as P

MESH = pl.DeviceIdType.MESH
BLOCK = 128
STEPS = 8
SUB = BLOCK // STEPS
LEVELS = 32767.0
TINY = 1e-30
TILE = 256
HALF = 1024
ORDER = (
    "E1L", "G0", "E2L", "G1", "E3L", "A0", "C0L", "A1", "C1L", "G2", "E1R", "G3",
    "A2", "C2L", "E2R", "G4", "G5", "A3", "C3L", "E3R", "C0R", "C1R", "C2R", "C3R",
    "G6", "G7", "A4", "C4L", "C4R", "A5", "C5L", "C5R", "D0", "D1", "A6", "C6L",
    "C6R", "D2", "D3", "Z0", "Z1", "Z2", "Z3", "A7", "C7L", "C7R", "D4", "Z4",
    "D5", "Z5", "D6", "Z6", "D7", "Z7", "F0", "F1", "F2", "F3", "F4", "F5",
    "F6", "F7",
)


def kernel(a_occ, b_occ, a_ref, b_ref, out_ref, a_slab, b_slab, part, sent, sent_scale, got, got_scale,
           held, z_sent, z_sent_scale, z_got, z_got_scale,
           a_plus, a_minus, a_recv, b_plus, b_minus, b_twin, b_recv, b_twin_recv,
           y_send, y_recv, y_send_s, y_recv_s, z_send, z_recv, z_send_s, z_recv_s):
    row, zl, layer = lax.axis_index("row"), lax.axis_index("col"), lax.axis_index("layer")
    x, core = row // 2, row % 2
    y, zh = layer // 2, layer % 2

    def x_peer(shift):
        return {"row": ((x + shift + 4) % 4) * 2 + core}

    twin = {"row": x * 2 + (1 - core)}

    def y_peer(shift):
        return {"layer": ((y + shift) % 4) * 2 + zh}

    z_peer = {"layer": y * 2 + (1 - zh)}

    barrier = pltpu.get_barrier_semaphore()
    greeted = [x_peer(1), x_peer(-1), twin, y_peer(1), y_peer(2), y_peer(3), z_peer]
    greeted += [{"col": (zl + 1) % 4}, {"col": (zl + 3) % 4}]
    for peer in greeted:
        pl.semaphore_signal(barrier, inc=1, device_id=peer, device_id_type=MESH)

    for i in range(8):
        for k in range(4):
            cols = pl.ds(k * BLOCK, BLOCK)
            flag = a_occ[k, i].astype(jnp.float32)
            kept = a_ref[i, :, :, cols].astype(jnp.float32) * flag
            a_slab[:, zl, i, :, cols] = kept.astype(jnp.bfloat16)
    for i in range(2):
        for j in range(16):
            cols = pl.ds(j * BLOCK, BLOCK)
            rows = pl.ds(i * BLOCK, BLOCK)
            flag = b_occ[i, j].astype(jnp.float32)
            kept = b_ref[rows, cols].astype(jnp.float32) * flag
            b_slab[row, i, j // 8, :, pl.ds(j % 8 * BLOCK, BLOCK)] = kept.astype(jnp.bfloat16)
    pl.semaphore_wait(barrier, len(greeted))

    def copy(src, dst, send, recv, peer):
        return pltpu.make_async_remote_copy(
            src_ref=src, dst_ref=dst, send_sem=send, recv_sem=recv, device_id=peer, device_id_type=MESH
        )

    def a_up(s, d):
        k = zl - d
        return copy(a_slab.at[s, k], a_slab.at[s, k], a_plus.at[s, d], a_recv.at[s, k], {"col": zl + 1})

    def a_down(s, d):
        k = zl + d
        return copy(a_slab.at[s, k], a_slab.at[s, k], a_minus.at[s, d], a_recv.at[s, k], {"col": zl - 1})

    def up_sends(d):
        return jnp.logical_and(zl >= d, zl < 3)

    def down_sends(d):
        return jnp.logical_and(zl + d <= 3, zl > 0)

    def a_own(s):
        pl.when(up_sends(0))(lambda: a_up(s, 0).start())
        pl.when(down_sends(0))(lambda: a_down(s, 0).start())

    def a_wait(s, d, sign):
        k = zl + sign * d
        copy(a_slab.at[s, k], a_slab.at[s, k], a_plus.at[s, 0], a_recv.at[s, k], {"col": zl}).wait_recv()

    def g_stage(s):
        for d in (1, 2):
            @pl.when(up_sends(d))
            def _():
                a_wait(s, d, -1)
                a_up(s, d).start()

            @pl.when(down_sends(d))
            def _():
                a_wait(s, d, 1)
                a_down(s, d).start()
        if s + 2 < STEPS:
            a_own(s + 2)

    def a_stage(s):
        for d in (1, 2, 3):
            for sign, sends in ((-1, up_sends), (1, down_sends)):
                here = jnp.logical_and(zl + sign * d >= 0, zl + sign * d <= 3)
                if d < 3:
                    here = jnp.logical_and(here, jnp.logical_not(sends(d)))
                pl.when(here)(lambda: a_wait(s, d, sign))

    def chunk(shift):
        return ((x + shift + 4) % 4) * 2 + core

    def b_copy(shift, h, q, sem, peer, recv):
        c = chunk(shift)
        return copy(b_slab.at[c, h, q], b_slab.at[c, h, q], sem, recv.at[c, h, q], peer)

    def b_to_plus(shift, h, q, n):
        return b_copy(shift, h, q, b_plus.at[q, n], x_peer(1), b_recv)

    def b_to_minus(shift, h, q, n):
        return b_copy(shift, h, q, b_minus.at[q, n], x_peer(-1), b_recv)

    def b_to_twin(shift, h, q):
        return b_copy(shift, h, q, b_twin.at[q, shift + 1, h], twin, b_twin_recv)

    def b_wait(shift, h, q):
        b_copy(shift, h, q, b_plus.at[q, 0], x_peer(1), b_recv).wait_recv()

    def b_own(q):
        for h in range(2):
            b_to_plus(0, h, q, h).start()
            b_to_minus(0, 1 - h, q, h).start()

    def e_stage(n, q):
        if n == 1:
            b_wait(-1, 0, q)
            b_to_plus(-1, 0, q, 2).start()
            b_wait(1, 1, q)
            b_to_minus(1, 1, q, 2).start()
            b_to_twin(-1, 0, q).start()
            b_to_twin(1, 1, q).start()
            if q == 0:
                b_own(1)
                for h in range(2):
                    b_to_twin(0, h, 1).start()
        elif n == 2:
            b_wait(-1, 1, q)
            b_to_twin(-1, 1, q).start()
            b_wait(1, 0, q)
            b_to_twin(1, 0, q).start()
        else:
            b_wait(2, 0, q)
            b_to_twin(2, 0, q).start()
            b_wait(2, 1, q)
            b_to_twin(2, 1, q).start()
            for other in range(4):
                for h in range(2):
                    c = other * 2 + 1 - core
                    copy(b_slab.at[c, h, q], b_slab.at[c, h, q], b_plus.at[q, 0], b_twin_recv.at[c, h, q],
                         twin).wait_recv()

    def y_data(s, q, shift):
        return copy(sent.at[s, q, (y + shift) % 4], got.at[s, q, shift - 1], y_send.at[s, q, shift - 1],
                    y_recv.at[s, q, shift - 1], y_peer(shift))

    def y_scale(s, q, shift):
        return copy(sent_scale.at[s, q], got_scale.at[s, q, shift - 1], y_send_s.at[s, q, shift - 1],
                    y_recv_s.at[s, q, shift - 1], y_peer(shift))

    def coded(values, axes):
        most = jnp.maximum(jnp.max(jnp.abs(values), axis=axes, keepdims=True), TINY)
        codes = jnp.round(values * (LEVELS / most)).astype(jnp.int16)
        return codes, most * (1.0 / LEVELS)

    def c_stage(s, q):
        @pl.loop(0, HALF // TILE)
        def _(n):
            cols = pl.ds(pl.multiple_of(n * TILE, TILE), TILE)
            total = jnp.zeros((BLOCK, TILE), jnp.float32)
            for k in range(4):
                total += jnp.dot(
                    a_slab[s, k].reshape(BLOCK, 512),
                    b_slab[2 * k:2 * k + 2, :, q, :, cols].reshape(512, TILE),
                    preferred_element_type=jnp.float32,
                )
            part[:, :, :, cols] = total.reshape(4, 2, SUB, TILE)
            codes, scale = coded(total, 0)
            sent[s, q, :, :, :, cols] = codes.reshape(4, 2, SUB, TILE)
            sent_scale[s, q, :, cols] = scale

        held[s, q] = part[y]
        for shift in (2, 1, 3):
            y_data(s, q, shift).start()
            y_scale(s, q, shift).start()

    def d_stage(s):
        for q in range(2):
            for shift in (2, 1, 3):
                y_data(s, q, shift).wait_recv()
                y_scale(s, q, shift).wait_recv()
            mine = held[s, q, zh]
            theirs = held[s, q, 1 - zh]
            for n in range(3):
                mine += got[s, q, n, zh].astype(jnp.float32) * got_scale[s, q, n]
                theirs += got[s, q, n, 1 - zh].astype(jnp.float32) * got_scale[s, q, n]
            held[s, q, zh] = mine
            codes, scale = coded(theirs, 0)
            z_sent[s, q] = codes
            z_sent_scale[s, q] = scale

    def z_data(s):
        return copy(z_sent.at[s], z_got.at[s], z_send.at[s], z_recv.at[s], z_peer)

    def z_scale(s):
        return copy(z_sent_scale.at[s], z_got_scale.at[s], z_send_s.at[s], z_recv_s.at[s], z_peer)

    def z_stage(s):
        z_data(s).start()
        z_scale(s).start()

    def f_stage(s):
        z_data(s).wait_recv()
        z_scale(s).wait_recv()
        for q in range(2):
            out_ref[s, :, q * HALF:(q + 1) * HALF] = (
                held[s, q, zh] + z_got[s, q].astype(jnp.float32) * z_got_scale[s, q]
            )

    a_own(0)
    b_own(0)
    a_own(1)
    for h in range(2):
        b_to_twin(0, h, 0).start()
    stages = {"A": a_stage, "C": c_stage, "D": d_stage, "E": e_stage, "F": f_stage, "G": g_stage, "Z": z_stage}
    for name in ORDER:
        halves = ("LR".index(name[2]),) if name[2:] else ()
        stages[name[0]](int(name[1]), *halves)

    for s in range(STEPS):
        for d in range(3):
            pl.when(up_sends(d))(lambda: a_up(s, d).wait_send())
            pl.when(down_sends(d))(lambda: a_down(s, d).wait_send())
        for q in range(2):
            for shift in (1, 2, 3):
                y_data(s, q, shift).wait_send()
                y_scale(s, q, shift).wait_send()
        z_data(s).wait_send()
        z_scale(s).wait_send()
    for q in range(2):
        for n in range(3):
            b_to_plus(0, 0, q, n).wait_send()
            b_to_minus(0, 0, q, n).wait_send()
        for shift in (-1, 0, 1, 2):
            for h in range(2):
                b_to_twin(shift, h, q).wait_send()


def per_device(a_tiles, a_occupancy, b_tiles, b_occupancy):
    vmem = pl.BlockSpec(memory_space=pltpu.VMEM)
    smem = pl.BlockSpec(memory_space=pltpu.SMEM)
    sems = pltpu.SemaphoreType.DMA
    out = pl.pallas_call(
        kernel,
        out_shape=jax.ShapeDtypeStruct((STEPS, SUB, 2048), jnp.float32),
        in_specs=[smem, smem, vmem, vmem],
        out_specs=vmem,
        scratch_shapes=[
            pltpu.VMEM((STEPS, 4, 8, SUB, 512), jnp.bfloat16),
            pltpu.VMEM((8, 2, 2, BLOCK, HALF), jnp.bfloat16),
            pltpu.VMEM((4, 2, SUB, HALF), jnp.float32),
            pltpu.VMEM((STEPS, 2, 4, 2, SUB, HALF), jnp.int16),
            pltpu.VMEM((STEPS, 2, 1, HALF), jnp.float32),
            pltpu.VMEM((STEPS, 2, 3, 2, SUB, HALF), jnp.int16),
            pltpu.VMEM((STEPS, 2, 3, 1, HALF), jnp.float32),
            pltpu.VMEM((STEPS, 2, 2, SUB, HALF), jnp.float32),
            pltpu.VMEM((STEPS, 2, SUB, HALF), jnp.int16),
            pltpu.VMEM((STEPS, 2, 1, HALF), jnp.float32),
            pltpu.VMEM((STEPS, 2, SUB, HALF), jnp.int16),
            pltpu.VMEM((STEPS, 2, 1, HALF), jnp.float32),
            sems((STEPS, 3)), sems((STEPS, 3)), sems((STEPS, 4)),
            sems((2, 3)), sems((2, 3)), sems((2, 4, 2)), sems((8, 2, 2)), sems((8, 2, 2)),
            sems((STEPS, 2, 3)), sems((STEPS, 2, 3)), sems((STEPS, 2, 3)), sems((STEPS, 2, 3)),
            sems((STEPS,)), sems((STEPS,)), sems((STEPS,)), sems((STEPS,)),
        ],
        compiler_params=pltpu.CompilerParams(
            collective_id=0, has_side_effects=True, vmem_limit_bytes=56 << 20
        ),
    )(a_occupancy.T, b_occupancy, a_tiles.reshape(8, STEPS, SUB, 512), b_tiles)
    return out.reshape(BLOCK, 2048)


def solution(mesh):
    in_specs = (
        P("row", ("layer", "col")),
        P("row", ("layer", "col")),
        P(("layer", "row"), "col"),
        P(("layer", "row"), "col"),
    )
    out_specs = P(("row", "layer"), "col")
    return jax.shard_map(
        per_device, mesh=mesh, in_specs=in_specs, out_specs=out_specs, check_vma=False
    )
```

```python
import functools

import jax
import jax.numpy as jnp
from jax import lax
from jax.experimental import pallas as pl
from jax.experimental.pallas import tpu as pltpu
from jax.sharding import PartitionSpec as P

MESH = pl.DeviceIdType.MESH
BLOCK = 128
STEPS = 8
SUB = BLOCK // STEPS
LEVELS = 32767.0
TINY = 1e-30
TILE = 256
HALF = 1024
ORDER = (
    "G0", "E1L", "G1", "E2L", "E3L", "A1", "G2", "A2", "A0", "C2L", "E1R", "C1L",
    "G3", "C0L", "E2R", "A3", "C3L", "E3R", "G4", "C0R", "C2R", "A4", "G5", "C3R",
    "C1R", "A5", "D0", "Z0", "C4R", "G6", "C4L", "C5L", "D3", "C5R", "Z3", "G7",
    "A6", "C6L", "D1", "D4", "D2", "Z1", "Z4", "C6R", "A7", "F3", "Z2", "C7L",
    "D5", "F0", "C7R", "D6", "Z5", "Z6", "F4", "D7", "Z7", "F6", "F1", "F2",
    "F5", "F7",
)


def kernel(a_occ, b_occ, a_ref, b_ref, out_ref, a_slab, b_slab, part, sent, sent_scale, got, got_scale,
           held, z_sent, z_sent_scale, z_got, z_got_scale,
           a_plus, a_minus, a_recv, b_plus, b_minus, b_twin, b_recv, b_twin_recv,
           y_send, y_recv, y_send_s, y_recv_s, z_send, z_recv, z_send_s, z_recv_s):
    row, zl, layer = lax.axis_index("row"), lax.axis_index("col"), lax.axis_index("layer")
    x, core = row // 2, row % 2
    y, zh = layer // 2, layer % 2

    def x_peer(shift):
        return {"row": ((x + shift + 4) % 4) * 2 + core}

    twin = {"row": x * 2 + (1 - core)}

    def y_peer(shift):
        return {"layer": ((y + shift) % 4) * 2 + zh}

    z_peer = {"layer": y * 2 + (1 - zh)}

    barrier = pltpu.get_barrier_semaphore()
    greeted = [x_peer(1), x_peer(-1), twin, y_peer(1), y_peer(2), y_peer(3), z_peer]
    greeted += [{"col": (zl + 1) % 4}, {"col": (zl + 3) % 4}]
    for peer in greeted:
        pl.semaphore_signal(barrier, inc=1, device_id=peer, device_id_type=MESH)

    for i in range(8):
        for k in range(4):
            cols = pl.ds(k * BLOCK, BLOCK)
            flag = a_occ[k, i].astype(jnp.float32)
            kept = a_ref[i, :, :, cols].astype(jnp.float32) * flag
            a_slab[:, zl, i, :, cols] = kept.astype(jnp.bfloat16)
    for i in range(2):
        for j in range(16):
            cols = pl.ds(j * BLOCK, BLOCK)
            rows = pl.ds(i * BLOCK, BLOCK)
            flag = b_occ[i, j].astype(jnp.float32)
            kept = b_ref[rows, cols].astype(jnp.float32) * flag
            b_slab[row, i, j // 8, :, pl.ds(j % 8 * BLOCK, BLOCK)] = kept.astype(jnp.bfloat16)
    pl.semaphore_wait(barrier, len(greeted))

    def copy(src, dst, send, recv, peer):
        return pltpu.make_async_remote_copy(
            src_ref=src, dst_ref=dst, send_sem=send, recv_sem=recv, device_id=peer, device_id_type=MESH
        )

    def a_up(s, d):
        k = zl - d
        return copy(a_slab.at[s, k], a_slab.at[s, k], a_plus.at[d], a_recv.at[s, k], {"col": zl + 1})

    def a_down(s, d):
        k = zl + d
        return copy(a_slab.at[s, k], a_slab.at[s, k], a_minus.at[d], a_recv.at[s, k], {"col": zl - 1})

    def up_sends(d):
        return jnp.logical_and(zl >= d, zl < 3)

    def down_sends(d):
        return jnp.logical_and(zl + d <= 3, zl > 0)

    def a_own(s):
        pl.when(up_sends(0))(lambda: a_up(s, 0).start())
        pl.when(down_sends(0))(lambda: a_down(s, 0).start())

    def a_wait(s, d, sign):
        k = zl + sign * d
        copy(a_slab.at[s, k], a_slab.at[s, k], a_plus.at[0], a_recv.at[s, k], {"col": zl}).wait_recv()

    def g_stage(s):
        for d in (1, 2):
            @pl.when(up_sends(d))
            def _():
                a_wait(s, d, -1)
                a_up(s, d).start()

            @pl.when(down_sends(d))
            def _():
                a_wait(s, d, 1)
                a_down(s, d).start()
        if s + 2 < STEPS:
            a_own(s + 2)

    def a_stage(s):
        for d in (1, 2, 3):
            for sign, sends in ((-1, up_sends), (1, down_sends)):
                here = jnp.logical_and(zl + sign * d >= 0, zl + sign * d <= 3)
                if d < 3:
                    here = jnp.logical_and(here, jnp.logical_not(sends(d)))
                pl.when(here)(lambda: a_wait(s, d, sign))

    def chunk(shift):
        return ((x + shift + 4) % 4) * 2 + core

    def b_copy(shift, h, q, sem, peer, recv):
        c = chunk(shift)
        return copy(b_slab.at[c, h, q], b_slab.at[c, h, q], sem, recv, peer)

    def b_to_plus(shift, h, q):
        return b_copy(shift, h, q, b_plus, x_peer(1), b_recv.at[(x + shift + 4) % 4, h, q])

    def b_to_minus(shift, h, q):
        return b_copy(shift, h, q, b_minus, x_peer(-1), b_recv.at[(x + shift + 4) % 4, h, q])

    def b_to_twin(shift, h, q):
        return b_copy(shift, h, q, b_twin, twin, b_twin_recv.at[q])

    def b_wait(shift, h, q):
        b_copy(shift, h, q, b_plus, x_peer(1), b_recv.at[(x + shift + 4) % 4, h, q]).wait_recv()

    def b_own(q):
        for h in range(2):
            b_to_plus(0, h, q).start()
            b_to_minus(0, 1 - h, q).start()

    def e_stage(n, q):
        if n == 1:
            b_wait(-1, 0, q)
            b_to_plus(-1, 0, q).start()
            b_wait(1, 1, q)
            b_to_minus(1, 1, q).start()
            b_to_twin(-1, 0, q).start()
            b_to_twin(1, 1, q).start()
            if q == 0:
                b_own(1)
                for h in range(2):
                    b_to_twin(0, h, 1).start()
        elif n == 2:
            b_wait(-1, 1, q)
            b_to_twin(-1, 1, q).start()
            b_wait(1, 0, q)
            b_to_twin(1, 0, q).start()
        else:
            b_wait(2, 0, q)
            b_to_twin(2, 0, q).start()
            b_wait(2, 1, q)
            b_to_twin(2, 1, q).start()
            eight = b_slab.at[0:4, :, 0]
            copy(eight, eight, b_plus, b_twin_recv.at[q], twin).wait_recv()

    def y_data(s, q, shift):
        return copy(sent.at[s, q, (y + shift) % 4], got.at[s, q, shift - 1], y_send,
                    y_recv.at[s], y_peer(shift))

    def y_scale(s, q, shift):
        return copy(sent_scale.at[s, q], got_scale.at[s, q, shift - 1], y_send_s,
                    y_recv_s.at[s], y_peer(shift))

    def coded(values, axes):
        most = jnp.maximum(jnp.max(jnp.abs(values), axis=axes, keepdims=True), TINY)
        codes = jnp.round(values * (LEVELS / most)).astype(jnp.int16)
        return codes, most * (1.0 / LEVELS)

    def c_stage(s, q):
        @pl.loop(0, HALF // TILE)
        def _(n):
            cols = pl.ds(pl.multiple_of(n * TILE, TILE), TILE)
            total = jnp.zeros((BLOCK, TILE), jnp.float32)
            for k in range(4):
                total += jnp.dot(
                    a_slab[s, k].reshape(BLOCK, 512),
                    b_slab[2 * k:2 * k + 2, :, q, :, cols].reshape(512, TILE),
                    preferred_element_type=jnp.float32,
                )
            part[:, :, :, cols] = total.reshape(4, 2, SUB, TILE)
            codes, scale = coded(total, 0)
            sent[s, q, :, :, :, cols] = codes.reshape(4, 2, SUB, TILE)
            sent_scale[s, q, :, cols] = scale

        held[s, q] = part[y]
        for shift in (2, 1, 3):
            y_data(s, q, shift).start()
            y_scale(s, q, shift).start()

    def d_stage(s):
        copy(got.at[s], got.at[s], y_send, y_recv.at[s], y_peer(1)).wait_recv()
        copy(got_scale.at[s], got_scale.at[s], y_send_s, y_recv_s.at[s], y_peer(1)).wait_recv()
        for q in range(2):
            mine = held[s, q, zh]
            theirs = held[s, q, 1 - zh]
            for n in range(3):
                mine += got[s, q, n, zh].astype(jnp.float32) * got_scale[s, q, n]
                theirs += got[s, q, n, 1 - zh].astype(jnp.float32) * got_scale[s, q, n]
            held[s, q, zh] = mine
            codes, scale = coded(theirs, 0)
            z_sent[s, q] = codes
            z_sent_scale[s, q] = scale

    def z_data(s):
        return copy(z_sent.at[s], z_got.at[s], z_send, z_recv.at[s], z_peer)

    def z_scale(s):
        return copy(z_sent_scale.at[s], z_got_scale.at[s], z_send_s, z_recv_s.at[s], z_peer)

    def z_stage(s):
        z_data(s).start()
        z_scale(s).start()

    def f_stage(s):
        z_data(s).wait_recv()
        z_scale(s).wait_recv()
        for q in range(2):
            out_ref[s, :, q * HALF:(q + 1) * HALF] = (
                held[s, q, zh] + z_got[s, q].astype(jnp.float32) * z_got_scale[s, q]
            )

    a_own(0)
    b_own(0)
    a_own(1)
    for h in range(2):
        b_to_twin(0, h, 0).start()
    stages = {"A": a_stage, "C": c_stage, "D": d_stage, "E": e_stage, "F": f_stage, "G": g_stage, "Z": z_stage}
    for name in ORDER:
        halves = ("LR".index(name[2]),) if name[2:] else ()
        stages[name[0]](int(name[1]), *halves)

    def all_left(ref, sem):
        copy(ref, ref, sem, z_recv.at[0], z_peer).wait_send()

    for d in range(3):
        pl.when(up_sends(d))(lambda: all_left(a_slab.at[:, 0], a_plus.at[d]))
        pl.when(down_sends(d))(lambda: all_left(a_slab.at[:, 0], a_minus.at[d]))
    all_left(b_slab.at[0:3, 0], b_plus)
    all_left(b_slab.at[0:3, 0], b_minus)
    all_left(b_slab.at[0:4], b_twin)
    all_left(got, y_send)
    all_left(got_scale, y_send_s)
    all_left(z_got, z_send)
    all_left(z_got_scale, z_send_s)


def per_device(a_tiles, a_occupancy, b_tiles, b_occupancy):
    vmem = pl.BlockSpec(memory_space=pltpu.VMEM)
    smem = pl.BlockSpec(memory_space=pltpu.SMEM)
    sems = pltpu.SemaphoreType.DMA
    out = pl.pallas_call(
        kernel,
        out_shape=jax.ShapeDtypeStruct((STEPS, SUB, 2048), jnp.float32),
        in_specs=[smem, smem, vmem, vmem],
        out_specs=vmem,
        scratch_shapes=[
            pltpu.VMEM((STEPS, 4, 8, SUB, 512), jnp.bfloat16),
            pltpu.VMEM((8, 2, 2, BLOCK, HALF), jnp.bfloat16),
            pltpu.VMEM((4, 2, SUB, HALF), jnp.float32),
            pltpu.VMEM((STEPS, 2, 4, 2, SUB, HALF), jnp.int16),
            pltpu.VMEM((STEPS, 2, 1, HALF), jnp.float32),
            pltpu.VMEM((STEPS, 2, 3, 2, SUB, HALF), jnp.int16),
            pltpu.VMEM((STEPS, 2, 3, 1, HALF), jnp.float32),
            pltpu.VMEM((STEPS, 2, 2, SUB, HALF), jnp.float32),
            pltpu.VMEM((STEPS, 2, SUB, HALF), jnp.int16),
            pltpu.VMEM((STEPS, 2, 1, HALF), jnp.float32),
            pltpu.VMEM((STEPS, 2, SUB, HALF), jnp.int16),
            pltpu.VMEM((STEPS, 2, 1, HALF), jnp.float32),
            sems((3,)), sems((3,)), sems((STEPS, 4)),
            sems, sems, sems, sems((4, 2, 2)), sems((2,)),
            sems, sems((STEPS,)), sems, sems((STEPS,)),
            sems, sems((STEPS,)), sems, sems((STEPS,)),
        ],
        compiler_params=pltpu.CompilerParams(
            collective_id=0, has_side_effects=True, vmem_limit_bytes=56 << 20
        ),
    )(a_occupancy.T, b_occupancy, a_tiles.reshape(8, STEPS, SUB, 512), b_tiles)
    return out.reshape(BLOCK, 2048)


def solution(mesh):
    in_specs = (
        P("row", ("layer", "col")),
        P("row", ("layer", "col")),
        P(("layer", "row"), "col"),
        P(("layer", "row"), "col"),
    )
    out_specs = P(("row", "layer"), "col")
    return jax.shard_map(
        per_device, mesh=mesh, in_specs=in_specs, out_specs=out_specs, check_vma=False
    )
```

```python
import functools

import jax
import jax.numpy as jnp
from jax import lax
from jax.experimental import pallas as pl
from jax.experimental.pallas import tpu as pltpu
from jax.sharding import PartitionSpec as P

MESH = pl.DeviceIdType.MESH
BLOCK = 128
STEPS = 8
SUB = BLOCK // STEPS
LEVELS = 32767.0
TINY = 1e-30
TILE = 256
HALF = 1024
ORDER = (
    "G0", "E1L", "G1", "E2L", "E3L", "A1", "G2", "A2", "A0", "C2L", "E1R", "C1L",
    "G3", "C0L", "E2R", "A3", "C3L", "E3R", "G4", "C0R", "C2R", "A4", "G5", "C3R",
    "C1R", "A5", "D0", "Z0", "C4R", "G6", "C4L", "C5L", "D3", "C5R", "Z3", "G7",
    "A6", "C6L", "D1", "D4", "D2", "Z1", "Z4", "C6R", "A7", "F3", "Z2", "C7L",
    "D5", "F0", "C7R", "D6", "Z5", "Z6", "F4", "D7", "Z7", "F6", "F1", "F2",
    "F5", "F7",
)


def kernel(a_occ, b_occ, a_ref, b_ref, out_ref, a_slab, b_slab, part, sent, sent_scale, got, got_scale,
           held, z_sent, z_sent_scale, z_got, z_got_scale,
           a_plus, a_minus, a_recv, b_plus, b_minus, b_twin, b_recv, b_twin_recv,
           y_send, y_recv, y_send_s, y_recv_s, z_send, z_recv, z_send_s, z_recv_s):
    row, zl, layer = lax.axis_index("row"), lax.axis_index("col"), lax.axis_index("layer")
    x, core = row // 2, row % 2
    y, zh = layer // 2, layer % 2

    def x_peer(shift):
        return {"row": ((x + shift + 4) % 4) * 2 + core}

    twin = {"row": x * 2 + (1 - core)}

    def y_peer(shift):
        return {"layer": ((y + shift) % 4) * 2 + zh}

    z_peer = {"layer": y * 2 + (1 - zh)}

    barrier = pltpu.get_barrier_semaphore()
    greeted = [x_peer(1), x_peer(-1), twin, y_peer(1), y_peer(2), y_peer(3), z_peer]
    greeted += [{"col": (zl + 1) % 4}, {"col": (zl + 3) % 4}]
    for peer in greeted:
        pl.semaphore_signal(barrier, inc=1, device_id=peer, device_id_type=MESH)

    for i in range(8):
        for k in range(4):
            cols = pl.ds(k * BLOCK, BLOCK)
            flag = a_occ[k, i].astype(jnp.float32)
            kept = a_ref[i, :, :, cols].astype(jnp.float32) * flag
            a_slab[:, zl, i, :, cols] = kept.astype(jnp.bfloat16)
    for i in range(2):
        for j in range(16):
            cols = pl.ds(j * BLOCK, BLOCK)
            rows = pl.ds(i * BLOCK, BLOCK)
            flag = b_occ[i, j].astype(jnp.float32)
            kept = b_ref[rows, cols].astype(jnp.float32) * flag
            b_slab[row, i, j // 8, :, pl.ds(j % 8 * BLOCK, BLOCK)] = kept.astype(jnp.bfloat16)
    pl.semaphore_wait(barrier, len(greeted))

    def copy(src, dst, send, recv, peer):
        return pltpu.make_async_remote_copy(
            src_ref=src, dst_ref=dst, send_sem=send, recv_sem=recv, device_id=peer, device_id_type=MESH
        )

    def a_up(s, d):
        k = zl - d
        return copy(a_slab.at[s, k], a_slab.at[s, k], a_plus.at[d], a_recv.at[s, k], {"col": zl + 1})

    def a_down(s, d):
        k = zl + d
        return copy(a_slab.at[s, k], a_slab.at[s, k], a_minus.at[d], a_recv.at[s, k], {"col": zl - 1})

    def up_sends(d):
        return jnp.logical_and(zl >= d, zl < 3)

    def down_sends(d):
        return jnp.logical_and(zl + d <= 3, zl > 0)

    def a_own(s):
        pl.when(up_sends(0))(lambda: a_up(s, 0).start())
        pl.when(down_sends(0))(lambda: a_down(s, 0).start())

    def a_wait(s, d, sign):
        k = zl + sign * d
        copy(a_slab.at[s, k], a_slab.at[s, k], a_plus.at[0], a_recv.at[s, k], {"col": zl}).wait_recv()

    def g_stage(s):
        for d in (1, 2):
            @pl.when(up_sends(d))
            def _():
                a_wait(s, d, -1)
                a_up(s, d).start()

            @pl.when(down_sends(d))
            def _():
                a_wait(s, d, 1)
                a_down(s, d).start()
        if s + 2 < STEPS:
            a_own(s + 2)

    def a_stage(s):
        for d in (1, 2, 3):
            for sign, sends in ((-1, up_sends), (1, down_sends)):
                here = jnp.logical_and(zl + sign * d >= 0, zl + sign * d <= 3)
                if d < 3:
                    here = jnp.logical_and(here, jnp.logical_not(sends(d)))
                pl.when(here)(lambda: a_wait(s, d, sign))

    def chunk(shift):
        return ((x + shift + 4) % 4) * 2 + core

    def b_copy(shift, h, q, sem, peer, recv):
        c = chunk(shift)
        return copy(b_slab.at[c, h, q], b_slab.at[c, h, q], sem, recv, peer)

    def b_to_plus(shift, h, q):
        return b_copy(shift, h, q, b_plus, x_peer(1), b_recv.at[(x + shift + 4) % 4, h, q])

    def b_to_minus(shift, h, q):
        return b_copy(shift, h, q, b_minus, x_peer(-1), b_recv.at[(x + shift + 4) % 4, h, q])

    def b_to_twin(shift, h, q):
        return b_copy(shift, h, q, b_twin, twin, b_twin_recv.at[q])

    def b_wait(shift, h, q):
        b_copy(shift, h, q, b_plus, x_peer(1), b_recv.at[(x + shift + 4) % 4, h, q]).wait_recv()

    def b_own(q):
        for h in range(2):
            b_to_plus(0, h, q).start()
            b_to_minus(0, 1 - h, q).start()

    def e_stage(n, q):
        if n == 1:
            b_wait(-1, 0, q)
            b_to_plus(-1, 0, q).start()
            b_wait(1, 1, q)
            b_to_minus(1, 1, q).start()
            b_to_twin(-1, 0, q).start()
            b_to_twin(1, 1, q).start()
            if q == 0:
                b_own(1)
                for h in range(2):
                    b_to_twin(0, h, 1).start()
        elif n == 2:
            b_wait(-1, 1, q)
            b_to_twin(-1, 1, q).start()
            b_wait(1, 0, q)
            b_to_twin(1, 0, q).start()
        else:
            b_wait(2, 0, q)
            b_to_twin(2, 0, q).start()
            b_wait(2, 1, q)
            b_to_twin(2, 1, q).start()
            eight = b_slab.at[0:4, :, 0]
            copy(eight, eight, b_plus, b_twin_recv.at[q], twin).wait_recv()

    def y_data(s, q, shift):
        return copy(sent.at[s, q, (y + shift) % 4], got.at[s, q, shift - 1], y_send,
                    y_recv.at[s], y_peer(shift))

    def y_scale(s, q, shift):
        return copy(sent_scale.at[s, q], got_scale.at[s, q, shift - 1], y_send_s,
                    y_recv_s.at[s], y_peer(shift))

    def coded(values, axes):
        most = jnp.maximum(jnp.max(jnp.abs(values), axis=axes, keepdims=True), TINY)
        codes = jnp.round(values * (LEVELS / most)).astype(jnp.int16)
        return codes, most * (1.0 / LEVELS)

    def c_stage(s, q):
        @pl.loop(0, HALF // TILE)
        def _(n):
            cols = pl.ds(pl.multiple_of(n * TILE, TILE), TILE)
            total = jnp.zeros((BLOCK, TILE), jnp.float32)
            for k in range(4):
                total += jnp.dot(
                    a_slab[s, k].reshape(BLOCK, 512),
                    b_slab[2 * k:2 * k + 2, :, q, :, cols].reshape(512, TILE),
                    preferred_element_type=jnp.float32,
                )
            part[:, :, :, cols] = total.reshape(4, 2, SUB, TILE)
            codes, scale = coded(total, 0)
            sent[s, q, :, :, :, cols] = codes.reshape(4, 2, SUB, TILE)
            sent_scale[s, q, :, cols] = scale

        held[s, q] = part[y]
        for shift in (2, 1, 3):
            y_data(s, q, shift).start()
            y_scale(s, q, shift).start()

    def d_stage(s):
        copy(got.at[s], got.at[s], y_send, y_recv.at[s], y_peer(1)).wait_recv()
        copy(got_scale.at[s], got_scale.at[s], y_send_s, y_recv_s.at[s], y_peer(1)).wait_recv()
        rest = []
        for q in range(2):
            mine = held[s, q, zh]
            theirs = held[s, q, 1 - zh]
            for n in range(3):
                mine += got[s, q, n, zh].astype(jnp.float32) * got_scale[s, q, n]
                theirs += got[s, q, n, 1 - zh].astype(jnp.float32) * got_scale[s, q, n]
            held[s, q, zh] = mine
            rest.append(theirs)
        most = jnp.max(jnp.maximum(jnp.abs(rest[0]), jnp.abs(rest[1])), axis=0, keepdims=True)
        lanes = [most[:, n * BLOCK:(n + 1) * BLOCK] for n in range(HALF // BLOCK)]
        peak = jnp.maximum(functools.reduce(jnp.maximum, lanes), TINY)
        wide = spread(LEVELS / peak)
        for q in range(2):
            z_sent[s, q] = jnp.round(rest[q] * wide).astype(jnp.int16)
        z_sent_scale[s] = peak * (1.0 / LEVELS)

    def spread(lanes):
        return jnp.concatenate([lanes] * (HALF // BLOCK), axis=1)

    def z_data(s):
        return copy(z_sent.at[s], z_got.at[s], z_send, z_recv.at[s], z_peer)

    def z_scale(s):
        return copy(z_sent_scale.at[s], z_got_scale.at[s], z_send_s, z_recv_s.at[s], z_peer)

    def z_stage(s):
        z_data(s).start()
        z_scale(s).start()

    def f_stage(s):
        z_data(s).wait_recv()
        z_scale(s).wait_recv()
        for q in range(2):
            out_ref[s, :, q * HALF:(q + 1) * HALF] = (
                held[s, q, zh] + z_got[s, q].astype(jnp.float32) * spread(z_got_scale[s])
            )

    a_own(0)
    b_own(0)
    a_own(1)
    for h in range(2):
        b_to_twin(0, h, 0).start()
    stages = {"A": a_stage, "C": c_stage, "D": d_stage, "E": e_stage, "F": f_stage, "G": g_stage, "Z": z_stage}
    for name in ORDER:
        halves = ("LR".index(name[2]),) if name[2:] else ()
        stages[name[0]](int(name[1]), *halves)

    def all_left(ref, sem):
        copy(ref, ref, sem, z_recv.at[0], z_peer).wait_send()

    for d in range(3):
        pl.when(up_sends(d))(lambda: all_left(a_slab.at[:, 0], a_plus.at[d]))
        pl.when(down_sends(d))(lambda: all_left(a_slab.at[:, 0], a_minus.at[d]))
    all_left(b_slab.at[0:3, 0], b_plus)
    all_left(b_slab.at[0:3, 0], b_minus)
    all_left(b_slab.at[0:4], b_twin)
    all_left(got, y_send)
    all_left(got_scale, y_send_s)
    all_left(z_got, z_send)
    all_left(z_got_scale, z_send_s)


def per_device(a_tiles, a_occupancy, b_tiles, b_occupancy):
    vmem = pl.BlockSpec(memory_space=pltpu.VMEM)
    smem = pl.BlockSpec(memory_space=pltpu.SMEM)
    sems = pltpu.SemaphoreType.DMA
    out = pl.pallas_call(
        kernel,
        out_shape=jax.ShapeDtypeStruct((STEPS, SUB, 2048), jnp.float32),
        in_specs=[smem, smem, vmem, vmem],
        out_specs=vmem,
        scratch_shapes=[
            pltpu.VMEM((STEPS, 4, 8, SUB, 512), jnp.bfloat16),
            pltpu.VMEM((8, 2, 2, BLOCK, HALF), jnp.bfloat16),
            pltpu.VMEM((4, 2, SUB, HALF), jnp.float32),
            pltpu.VMEM((STEPS, 2, 4, 2, SUB, HALF), jnp.int16),
            pltpu.VMEM((STEPS, 2, 1, HALF), jnp.float32),
            pltpu.VMEM((STEPS, 2, 3, 2, SUB, HALF), jnp.int16),
            pltpu.VMEM((STEPS, 2, 3, 1, HALF), jnp.float32),
            pltpu.VMEM((STEPS, 2, 2, SUB, HALF), jnp.float32),
            pltpu.VMEM((STEPS, 2, SUB, HALF), jnp.int16),
            pltpu.VMEM((STEPS, 1, BLOCK), jnp.float32),
            pltpu.VMEM((STEPS, 2, SUB, HALF), jnp.int16),
            pltpu.VMEM((STEPS, 1, BLOCK), jnp.float32),
            sems((3,)), sems((3,)), sems((STEPS, 4)),
            sems, sems, sems, sems((4, 2, 2)), sems((2,)),
            sems, sems((STEPS,)), sems, sems((STEPS,)),
            sems, sems((STEPS,)), sems, sems((STEPS,)),
        ],
        compiler_params=pltpu.CompilerParams(
            collective_id=0, has_side_effects=True, vmem_limit_bytes=56 << 20
        ),
    )(a_occupancy.T, b_occupancy, a_tiles.reshape(8, STEPS, SUB, 512), b_tiles)
    return out.reshape(BLOCK, 2048)


def solution(mesh):
    in_specs = (
        P("row", ("layer", "col")),
        P("row", ("layer", "col")),
        P(("layer", "row"), "col"),
        P(("layer", "row"), "col"),
    )
    out_specs = P(("row", "layer"), "col")
    return jax.shard_map(
        per_device, mesh=mesh, in_specs=in_specs, out_specs=out_specs, check_vma=False
    )
```

```python
import functools

import jax
import jax.numpy as jnp
from jax import lax
from jax.experimental import pallas as pl
from jax.experimental.pallas import tpu as pltpu
from jax.sharding import PartitionSpec as P

MESH = pl.DeviceIdType.MESH
BLOCK = 128
STEPS = 8
SUB = BLOCK // STEPS
LEVELS = 32767.0
TINY = 1e-30
TILE = 256
HALF = 1024
ORDER = (
    "G0", "E1L", "G1", "E2L", "E3L", "A1", "G2", "A2", "A0", "C2L", "E1R", "C1L",
    "G3", "C0L", "E2R", "A3", "C3L", "E3R", "G4", "C0R", "C2R", "A4", "G5", "C3R",
    "C1R", "A5", "D0", "Z0", "C4R", "G6", "C4L", "C5L", "D3", "C5R", "Z3", "G7",
    "A6", "C6L", "D1", "D4", "D2", "Z1", "Z4", "C6R", "A7", "Z2", "C7L", "D5",
    "Z5", "C7R", "D6", "Z6", "D7", "Z7", "F0", "F3", "F1", "F2", "F4", "F5",
    "F6", "F7",
)


def kernel(a_occ, b_occ, a_ref, b_ref, out_ref, a_slab, b_slab, part, sent, sent_scale, got, got_scale,
           held, z_sent, z_sent_scale, z_got, z_got_scale,
           a_plus, a_minus, a_recv, b_plus, b_minus, b_twin, b_recv, b_twin_recv,
           y_send, y_recv, y_send_s, y_recv_s, z_send, z_recv, z_send_s, z_recv_s):
    row, zl, layer = lax.axis_index("row"), lax.axis_index("col"), lax.axis_index("layer")
    x, core = row // 2, row % 2
    y, zh = layer // 2, layer % 2

    def x_peer(shift):
        return {"row": ((x + shift + 4) % 4) * 2 + core}

    twin = {"row": x * 2 + (1 - core)}

    def y_peer(shift):
        return {"layer": ((y + shift) % 4) * 2 + zh}

    z_peer = {"layer": y * 2 + (1 - zh)}

    barrier = pltpu.get_barrier_semaphore()
    greeted = [x_peer(1), x_peer(-1), twin, y_peer(1), y_peer(2), y_peer(3), z_peer]
    greeted += [{"col": (zl + 1) % 4}, {"col": (zl + 3) % 4}]
    for peer in greeted:
        pl.semaphore_signal(barrier, inc=1, device_id=peer, device_id_type=MESH)

    for i in range(8):
        for k in range(4):
            cols = pl.ds(k * BLOCK, BLOCK)
            flag = a_occ[k, i].astype(jnp.float32)
            kept = a_ref[i, :, :, cols].astype(jnp.float32) * flag
            a_slab[:, zl, i, :, cols] = kept.astype(jnp.bfloat16)
    for i in range(2):
        for j in range(16):
            cols = pl.ds(j * BLOCK, BLOCK)
            rows = pl.ds(i * BLOCK, BLOCK)
            flag = b_occ[i, j].astype(jnp.float32)
            kept = b_ref[rows, cols].astype(jnp.float32) * flag
            b_slab[row, i, j // 8, :, pl.ds(j % 8 * BLOCK, BLOCK)] = kept.astype(jnp.bfloat16)
    pl.semaphore_wait(barrier, len(greeted))

    def copy(src, dst, send, recv, peer):
        return pltpu.make_async_remote_copy(
            src_ref=src, dst_ref=dst, send_sem=send, recv_sem=recv, device_id=peer, device_id_type=MESH
        )

    def a_up(s, d):
        k = zl - d
        return copy(a_slab.at[s, k], a_slab.at[s, k], a_plus.at[d], a_recv.at[s, k], {"col": zl + 1})

    def a_down(s, d):
        k = zl + d
        return copy(a_slab.at[s, k], a_slab.at[s, k], a_minus.at[d], a_recv.at[s, k], {"col": zl - 1})

    def up_sends(d):
        return jnp.logical_and(zl >= d, zl < 3)

    def down_sends(d):
        return jnp.logical_and(zl + d <= 3, zl > 0)

    def a_own(s):
        pl.when(up_sends(0))(lambda: a_up(s, 0).start())
        pl.when(down_sends(0))(lambda: a_down(s, 0).start())

    def a_wait(s, d, sign):
        k = zl + sign * d
        copy(a_slab.at[s, k], a_slab.at[s, k], a_plus.at[0], a_recv.at[s, k], {"col": zl}).wait_recv()

    def g_stage(s):
        for d in (1, 2):
            @pl.when(up_sends(d))
            def _():
                a_wait(s, d, -1)
                a_up(s, d).start()

            @pl.when(down_sends(d))
            def _():
                a_wait(s, d, 1)
                a_down(s, d).start()
        if s + 3 < STEPS:
            a_own(s + 3)

    def a_stage(s):
        for d in (1, 2, 3):
            for sign, sends in ((-1, up_sends), (1, down_sends)):
                here = jnp.logical_and(zl + sign * d >= 0, zl + sign * d <= 3)
                if d < 3:
                    here = jnp.logical_and(here, jnp.logical_not(sends(d)))
                pl.when(here)(lambda: a_wait(s, d, sign))

    def chunk(shift):
        return ((x + shift + 4) % 4) * 2 + core

    def b_copy(shift, h, q, sem, peer, recv):
        c = chunk(shift)
        return copy(b_slab.at[c, h, q], b_slab.at[c, h, q], sem, recv, peer)

    def b_to_plus(shift, h, q):
        return b_copy(shift, h, q, b_plus, x_peer(1), b_recv.at[(x + shift + 4) % 4, h, q])

    def b_to_minus(shift, h, q):
        return b_copy(shift, h, q, b_minus, x_peer(-1), b_recv.at[(x + shift + 4) % 4, h, q])

    def b_to_twin(shift, h, q):
        return b_copy(shift, h, q, b_twin, twin, b_twin_recv.at[q])

    def b_wait(shift, h, q):
        b_copy(shift, h, q, b_plus, x_peer(1), b_recv.at[(x + shift + 4) % 4, h, q]).wait_recv()

    def b_own(q):
        for h in range(2):
            b_to_plus(0, h, q).start()
            b_to_minus(0, 1 - h, q).start()

    def e_stage(n, q):
        if n == 1:
            b_wait(-1, 0, q)
            b_to_plus(-1, 0, q).start()
            b_wait(1, 1, q)
            b_to_minus(1, 1, q).start()
            b_to_twin(-1, 0, q).start()
            b_to_twin(1, 1, q).start()
            if q == 0:
                b_own(1)
                for h in range(2):
                    b_to_twin(0, h, 1).start()
        elif n == 2:
            b_wait(-1, 1, q)
            b_to_twin(-1, 1, q).start()
            b_wait(1, 0, q)
            b_to_twin(1, 0, q).start()
        else:
            b_wait(2, 0, q)
            b_to_twin(2, 0, q).start()
            b_wait(2, 1, q)
            b_to_twin(2, 1, q).start()
            eight = b_slab.at[0:4, :, 0]
            copy(eight, eight, b_plus, b_twin_recv.at[q], twin).wait_recv()

    def y_data(s, q, shift):
        return copy(sent.at[s, q, (y + shift) % 4], got.at[s, q, shift - 1], y_send,
                    y_recv.at[s], y_peer(shift))

    def y_scale(s, q, shift):
        return copy(sent_scale.at[s, q], got_scale.at[s, q, shift - 1], y_send_s,
                    y_recv_s.at[s], y_peer(shift))

    def coded(values, axes):
        most = jnp.maximum(jnp.max(jnp.abs(values), axis=axes, keepdims=True), TINY)
        codes = jnp.round(values * (LEVELS / most)).astype(jnp.int16)
        return codes, most * (1.0 / LEVELS)

    def c_stage(s, q):
        @pl.loop(0, HALF // TILE)
        def _(n):
            cols = pl.ds(pl.multiple_of(n * TILE, TILE), TILE)
            total = jnp.zeros((BLOCK, TILE), jnp.float32)
            for k in range(4):
                total += jnp.dot(
                    a_slab[s, k].reshape(BLOCK, 512),
                    b_slab[2 * k:2 * k + 2, :, q, :, cols].reshape(512, TILE),
                    preferred_element_type=jnp.float32,
                )
            part[:, :, :, cols] = total.reshape(4, 2, SUB, TILE)
            codes, scale = coded(total, 0)
            sent[s, q, :, :, :, cols] = codes.reshape(4, 2, SUB, TILE)
            sent_scale[s, q, :, cols] = scale

        held[s, q] = part[y]
        for shift in (2, 1, 3):
            y_data(s, q, shift).start()
            y_scale(s, q, shift).start()

    def d_stage(s):
        copy(got.at[s], got.at[s], y_send, y_recv.at[s], y_peer(1)).wait_recv()
        copy(got_scale.at[s], got_scale.at[s], y_send_s, y_recv_s.at[s], y_peer(1)).wait_recv()
        rest = []
        for q in range(2):
            mine = held[s, q, zh]
            theirs = held[s, q, 1 - zh]
            for n in range(3):
                mine += got[s, q, n, zh].astype(jnp.float32) * got_scale[s, q, n]
                theirs += got[s, q, n, 1 - zh].astype(jnp.float32) * got_scale[s, q, n]
            held[s, q, zh] = mine
            rest.append(theirs)
        most = jnp.max(jnp.maximum(jnp.abs(rest[0]), jnp.abs(rest[1])), axis=0, keepdims=True)
        lanes = [most[:, n * BLOCK:(n + 1) * BLOCK] for n in range(HALF // BLOCK)]
        peak = jnp.maximum(functools.reduce(jnp.maximum, lanes), TINY)
        wide = spread(LEVELS / peak)
        for q in range(2):
            z_sent[s, q] = jnp.round(rest[q] * wide).astype(jnp.int16)
        z_sent_scale[s] = peak * (1.0 / LEVELS)

    def spread(lanes):
        return jnp.concatenate([lanes] * (HALF // BLOCK), axis=1)

    def z_data(s):
        return copy(z_sent.at[s], z_got.at[s], z_send, z_recv.at[s], z_peer)

    def z_scale(s):
        return copy(z_sent_scale.at[s], z_got_scale.at[s], z_send_s, z_recv_s.at[s], z_peer)

    def z_stage(s):
        z_data(s).start()
        z_scale(s).start()

    def f_stage(s):
        z_data(s).wait_recv()
        z_scale(s).wait_recv()
        for q in range(2):
            out_ref[s, :, q * HALF:(q + 1) * HALF] = (
                held[s, q, zh] + z_got[s, q].astype(jnp.float32) * spread(z_got_scale[s])
            )

    a_own(0)
    b_own(0)
    a_own(1)
    a_own(2)
    for h in range(2):
        b_to_twin(0, h, 0).start()
    stages = {"A": a_stage, "C": c_stage, "D": d_stage, "E": e_stage, "F": f_stage, "G": g_stage, "Z": z_stage}
    for name in ORDER:
        halves = ("LR".index(name[2]),) if name[2:] else ()
        stages[name[0]](int(name[1]), *halves)

    def all_left(ref, sem):
        copy(ref, ref, sem, z_recv.at[0], z_peer).wait_send()

    for d in range(3):
        pl.when(up_sends(d))(lambda: all_left(a_slab.at[:, 0], a_plus.at[d]))
        pl.when(down_sends(d))(lambda: all_left(a_slab.at[:, 0], a_minus.at[d]))
    all_left(b_slab.at[0:3, 0], b_plus)
    all_left(b_slab.at[0:3, 0], b_minus)
    all_left(b_slab.at[0:4], b_twin)
    all_left(got, y_send)
    all_left(got_scale, y_send_s)
    all_left(z_got, z_send)
    all_left(z_got_scale, z_send_s)


def per_device(a_tiles, a_occupancy, b_tiles, b_occupancy):
    vmem = pl.BlockSpec(memory_space=pltpu.VMEM)
    smem = pl.BlockSpec(memory_space=pltpu.SMEM)
    sems = pltpu.SemaphoreType.DMA
    out = pl.pallas_call(
        kernel,
        out_shape=jax.ShapeDtypeStruct((STEPS, SUB, 2048), jnp.float32),
        in_specs=[smem, smem, vmem, vmem],
        out_specs=vmem,
        scratch_shapes=[
            pltpu.VMEM((STEPS, 4, 8, SUB, 512), jnp.bfloat16),
            pltpu.VMEM((8, 2, 2, BLOCK, HALF), jnp.bfloat16),
            pltpu.VMEM((4, 2, SUB, HALF), jnp.float32),
            pltpu.VMEM((STEPS, 2, 4, 2, SUB, HALF), jnp.int16),
            pltpu.VMEM((STEPS, 2, 1, HALF), jnp.float32),
            pltpu.VMEM((STEPS, 2, 3, 2, SUB, HALF), jnp.int16),
            pltpu.VMEM((STEPS, 2, 3, 1, HALF), jnp.float32),
            pltpu.VMEM((STEPS, 2, 2, SUB, HALF), jnp.float32),
            pltpu.VMEM((STEPS, 2, SUB, HALF), jnp.int16),
            pltpu.VMEM((STEPS, 1, BLOCK), jnp.float32),
            pltpu.VMEM((STEPS, 2, SUB, HALF), jnp.int16),
            pltpu.VMEM((STEPS, 1, BLOCK), jnp.float32),
            sems((3,)), sems((3,)), sems((STEPS, 4)),
            sems, sems, sems, sems((4, 2, 2)), sems((2,)),
            sems, sems((STEPS,)), sems, sems((STEPS,)),
            sems, sems((STEPS,)), sems, sems((STEPS,)),
        ],
        compiler_params=pltpu.CompilerParams(
            collective_id=0, has_side_effects=True, vmem_limit_bytes=56 << 20
        ),
    )(a_occupancy.T, b_occupancy, a_tiles.reshape(8, STEPS, SUB, 512), b_tiles)
    return out.reshape(BLOCK, 2048)


def solution(mesh):
    in_specs = (
        P("row", ("layer", "col")),
        P("row", ("layer", "col")),
        P(("layer", "row"), "col"),
        P(("layer", "row"), "col"),
    )
    out_specs = P(("row", "layer"), "col")
    return jax.shard_map(
        per_device, mesh=mesh, in_specs=in_specs, out_specs=out_specs, check_vma=False
    )
```
